512 devices in a mesh: pair: 128 (over z, x_hi, y), virt: 4 (over x_lo, core).
Axes of the slice: x: 4 (x_hi: 2, x_lo: 2; x = x_hi * 2 + x_lo), y: 4, z: 16, core: 2. Of those that a mesh axis runs over, the one named last changes fastest.
Arguments:
- amplitudes: float32 [1024, 256, 256], P('pair', 'virt'), may hold values from -6 to 6
- fock_virtual: float32 [256, 256], P('virt'), may hold values from -0.375 to 0.375
- hole_ladder: float32 [1024, 1024], P(('pair', 'virt')), may hold values from -0.1875 to 0.1875
- occupied_energy: float32 [32], replicated, may hold values from -3 to -0.5
- virtual_energy: float32 [256], replicated, may hold values from 0.5 to 4
Outputs:
- update: float32 [1024, 256, 256], P('pair', 'virt')
The draws below stay inside these ranges and needn't reach their ends.
All inputs are finite; a program needn't handle non-finite values.
Results may differ from the reference program's by a relative error of at most 0.00007.
Values sent between devices are 32-bit elements; how exact they have to be, the bound alone decides.
No kernel may reach another device: no remote copies, remote signals or barrier semaphores. Data moves between devices by JAX's collectives and lax.ppermute only.
A program may use at most 64 MiB of HBM per device.

```python
import jax
import jax.numpy as jnp
from jax import lax

VIRT = 256
OCC = 32
PAIRS = 1024


def steps_of(rng, dims, cuts, low, top_value):
    def one(dim, parts):
        draws = jax.random.uniform(jax.random.fold_in(jax.random.fold_in(rng, 6), dim), (parts,), jnp.float32, low / len(cuts), top_value / len(cuts))
        return jnp.repeat(jnp.exp(draws), dims[dim] // parts).reshape((-1,) + (1,) * (len(dims) - dim - 1))

    loudness = one(*cuts[0])
    for cut in cuts[1:]:
        loudness = loudness * one(*cut)
    return loudness


def normal_values(key, extent, deviation, limit, pieces=(), kind=jnp.bfloat16):
    array = jax.random.normal(key, extent, jnp.float32) * deviation
    if len(pieces) > 0:
        array = steps_of(key, extent, pieces, -0.22, 0.18) * array
    return jnp.clip(array, min=-limit, max=limit).astype(kind)


def setup_inputs(seed: int = 0) -> dict:
    key_list = jax.random.split(jax.random.key(seed), 6)
    return {
        "amplitudes": normal_values(key_list[0], (PAIRS, VIRT, VIRT), 1.0, 6.0, ((0, 128), (1, 4)), jnp.float32),
        "fock_virtual": normal_values(key_list[1], (VIRT, VIRT), VIRT ** -0.5, 0.375, ((0, 4),), jnp.float32),
        "hole_ladder": normal_values(key_list[2], (PAIRS, PAIRS), PAIRS ** -0.5, 0.1875, ((0, 512),), jnp.float32),
        "occupied_energy": jnp.clip(jax.random.uniform(key_list[3], (OCC,), jnp.float32, -3.0, -0.5), -3.0, -0.5),
        "virtual_energy": jnp.clip(jax.random.uniform(key_list[4], (VIRT,), jnp.float32, 0.5, 4.0), 0.5, 4.0),
    }


PRECISE = lax.Precision.HIGHEST


def reference(amplitudes, fock_virtual, hole_ladder, occupied_energy, virtual_energy):
    amplitude_cube = amplitudes.reshape(OCC, OCC, VIRT, VIRT)
    combined = 2.0 * amplitude_cube - jnp.transpose(amplitude_cube, (1, 0, 2, 3))
    flattened = combined.reshape(OCC * OCC, VIRT * VIRT)
    ladder_blocks = hole_ladder.reshape(OCC, OCC, OCC * OCC)

    def one_row(row_index):
        pair_block = combined[row_index]
        first_term = jnp.einsum('ac,pcb->pab', fock_virtual, pair_block, precision=PRECISE, preferred_element_type=jnp.float32)
        second_term = jnp.einsum('pad,bd->pab', pair_block, fock_virtual, precision=PRECISE, preferred_element_type=jnp.float32)
        hole_term = jnp.dot(ladder_blocks[row_index], flattened, precision=PRECISE, preferred_element_type=jnp.float32).reshape(OCC, VIRT, VIRT)
        denominator = (occupied_energy[row_index] + occupied_energy)[:, None, None] - virtual_energy[None, :, None] - virtual_energy[None, None, :]
        return (first_term + second_term + hole_term) / denominator

    scaled = lax.map(one_row, jnp.arange(OCC, dtype=jnp.int32))
    return scaled.reshape(OCC * OCC, VIRT, VIRT)
```

```python
import jax
import jax.numpy as jnp
from jax import lax
from jax.sharding import Mesh, PartitionSpec as P

PRECISE = lax.Precision.HIGHEST
FAST = lax.Precision.HIGH
PAIR = ("z", "xh", "y")
SWAP = [(0, 1), (1, 0)]


def dot(a, b, dims, precision):
    return lax.dot_general(a, b, dims, precision=precision, preferred_element_type=jnp.float32)


def mirror(grouped, occupied):
    columns = grouped.shape[1]
    shaped = grouped.reshape(occupied, occupied, columns)
    return (2.0 * shaped - jnp.transpose(shaped, (1, 0, 2))).reshape(occupied * occupied, columns)


def flip_if(flag, first, second):
    return jnp.where(flag, second, first), jnp.where(flag, first, second)


def shards(amplitudes, fock_virtual, hole_ladder, occupied_energy, virtual_energy):
    pair_count, slab_width, full_width = amplitudes.shape
    occupied = occupied_energy.shape[0]
    pairs = occupied * occupied
    zs, xhs, ys = lax.axis_size("z"), lax.axis_size("xh"), lax.axis_size("y")
    at_xl, at_core = lax.axis_index("xl"), lax.axis_index("core")
    ladder = lax.all_gather(hole_ladder, ("y", "z", "xh", "xl", "core"), axis=0, tiled=True)

    flattened = amplitudes.reshape(pair_count, slab_width * full_width)
    grouped = lax.all_to_all(flattened, PAIR, split_axis=1, concat_axis=0, tiled=True)
    combined = mirror(grouped, occupied)
    combined_local = lax.all_to_all(combined, PAIR, split_axis=0, concat_axis=1, tiled=True)
    combined_local = combined_local.reshape(pair_count, slab_width, full_width)

    packed = jnp.concatenate([combined_local, fock_virtual[None]], axis=0)
    packed_c = lax.ppermute(packed, "core", SWAP)
    packed_x = lax.ppermute(packed, "xl", SWAP)
    packed_xc = lax.ppermute(packed_x, "core", SWAP)

    hole = dot(ladder, combined, (((1,), (0,)), ((), ())), FAST)
    hole = hole.reshape(ys, zs * xhs, pair_count, -1).transpose(1, 0, 2, 3).reshape(pairs, -1)
    hole_local = lax.all_to_all(hole, PAIR, split_axis=0, concat_axis=1, tiled=True)
    hole_local = hole_local.reshape(pair_count, slab_width, full_width)

    near = flip_if(at_core == 1, packed, packed_c)
    far = flip_if(at_core == 1, packed_x, packed_xc)
    low0, high0 = flip_if(at_xl == 1, near[0], far[0])
    low1, high1 = flip_if(at_xl == 1, near[1], far[1])
    whole = jnp.concatenate([low0, low1, high0, high1], axis=1)
    fock_full = whole[pair_count]
    first_term = dot(
        jnp.broadcast_to(fock_virtual, (pair_count,) + fock_virtual.shape),
        whole[:pair_count],
        (((2,), (1,)), ((0,), (0,))),
        FAST,
    )
    second_term = dot(combined_local, fock_full, (((2,), (1,)), ((), ())), FAST)
    residual = first_term + second_term + hole_local

    pair_base = lax.axis_index(PAIR) * pair_count
    pair_ids = pair_base + jnp.arange(pair_count, dtype=jnp.int32)
    orbital_ids = jnp.arange(occupied, dtype=jnp.int32)
    left_pick = pair_ids[:, None] // occupied == orbital_ids[None, :]
    right_pick = pair_ids[:, None] % occupied == orbital_ids[None, :]
    left_energy = jnp.sum(jnp.where(left_pick, occupied_energy[None, :], jnp.float32(0.0)), axis=1)
    right_energy = jnp.sum(
        jnp.where(right_pick, occupied_energy[None, :], jnp.float32(0.0)), axis=1
    )
    slab_energy = lax.dynamic_slice_in_dim(
        virtual_energy, lax.axis_index(("xl", "core")) * slab_width, slab_width
    )
    denominator = (
        (left_energy + right_energy)[:, None, None]
        - slab_energy[None, :, None]
        - virtual_energy[None, None, :]
    )
    return residual / denominator


def solution(mesh):
    fine = Mesh(
        mesh.devices.reshape(16, 2, 4, 2, 2), ("z", "xh", "y", "xl", "core")
    )
    virt = ("xl", "core")
    return jax.shard_map(
        shards,
        mesh=fine,
        in_specs=(P(PAIR, virt, None), P(virt, None), P(PAIR + virt, None), P(), P()),
        out_specs=P(PAIR, virt, None),
        check_vma=False,
    )
```

```python
import jax
import jax.numpy as jnp
from jax import lax
from jax.experimental import pallas as pl
from jax.experimental.pallas import tpu as pltpu
from jax.sharding import Mesh, PartitionSpec as P

PRECISE = lax.Precision.HIGHEST
FAST = lax.Precision.HIGH
PAIR = ("z", "xh", "y")
SWAP = [(0, 1), (1, 0)]


def dot(a, b, dims, precision):
    return lax.dot_general(a, b, dims, precision=precision, preferred_element_type=jnp.float32)


def mirror(grouped, occupied):
    columns = grouped.shape[1]
    shaped = grouped.reshape(occupied, occupied, columns)
    return (2.0 * shaped - jnp.transpose(shaped, (1, 0, 2))).reshape(occupied * occupied, columns)


def flip_if(flag, first, second):
    return jnp.where(flag, second, first), jnp.where(flag, first, second)


def split(value):
    high = value.astype(jnp.bfloat16)
    return high, (value - high.astype(jnp.float32)).astype(jnp.bfloat16)


def hole_kernel(order_ref, own_ref, other_ref, combined_ref, out_ref, high_ref, low_ref):
    chunks = own_ref.shape[0]
    depth = own_ref.shape[2]
    for k in range(chunks):
        start = pl.multiple_of(order_ref[k] * depth, depth)
        high, low = split(combined_ref[pl.ds(start, depth), :])
        high_ref[k * depth : (k + 1) * depth, :] = high
        low_ref[k * depth : (k + 1) * depth, :] = low
    for half, ref in enumerate((own_ref, other_ref)):
        rows = jnp.concatenate([ref[k] for k in range(chunks)], axis=1)
        high, low = split(rows)
        total = jnp.dot(low, high_ref[...], preferred_element_type=jnp.float32)
        total += jnp.dot(high, low_ref[...], preferred_element_type=jnp.float32)
        total += jnp.dot(high, high_ref[...], preferred_element_type=jnp.float32)
        out_ref[half] = total


def hole_rows(order, own, other, combined):
    chunks, rows, depth = own.shape
    columns = combined.shape[1]
    vmem = pl.BlockSpec(memory_space=pltpu.VMEM)
    flops = 12 * rows * chunks * depth * columns
    return pl.pallas_call(
        hole_kernel,
        out_shape=jax.ShapeDtypeStruct((2, rows, columns), jnp.float32),
        in_specs=[pl.BlockSpec(memory_space=pltpu.SMEM), vmem, vmem, vmem],
        out_specs=vmem,
        scratch_shapes=[pltpu.VMEM((chunks * depth, columns), jnp.bfloat16)] * 2,
        cost_estimate=pl.CostEstimate(
            flops=flops, bytes_accessed=4 * (2 * own.size + combined.size), transcendentals=0
        ),
    )(order, own, other, combined)


def shards(amplitudes, fock_virtual, hole_ladder, occupied_energy, virtual_energy):
    pair_count, slab_width, full_width = amplitudes.shape
    occupied = occupied_energy.shape[0]
    pairs = occupied * occupied
    zs, xhs, ys = lax.axis_size("z"), lax.axis_size("xh"), lax.axis_size("y")
    plane = xhs * ys
    groups = zs * plane
    at_xh, at_y = lax.axis_index("xh"), lax.axis_index("y")
    at_xl, at_core = lax.axis_index("xl"), lax.axis_index("core")
    columns = slab_width * full_width // groups
    ladder_rows = hole_ladder.shape[0]
    depth = pairs // plane

    outgoing = amplitudes.reshape(pair_count, groups, columns).transpose(1, 0, 2)
    outgoing = outgoing.reshape(groups, pair_count * columns)
    rungs = hole_ladder.reshape(ladder_rows, plane, depth).transpose(1, 0, 2)
    rungs = jnp.tile(rungs.reshape(plane, ladder_rows * depth), (zs, 1))
    sent = jnp.concatenate([outgoing, rungs], axis=1)[:, None, :]
    arrived = lax.all_to_all(sent, PAIR, split_axis=0, concat_axis=0, tiled=True)[:, 0, :]
    grouped = arrived[:, : pair_count * columns].reshape(pairs, columns)
    rungs = arrived[:, pair_count * columns :].reshape(groups, ladder_rows, depth)
    rungs = rungs.transpose(1, 0, 2).reshape(ladder_rows * groups, depth)

    both = jnp.stack([rungs, lax.ppermute(rungs, "xh", SWAP)])
    shift = lambda by: [(i, (i + by) % ys) for i in range(ys)]
    quads = [both] + [lax.ppermute(both, "y", shift(by)) for by in (1, ys - 1, 2)]
    own = jnp.concatenate(quads, axis=0)
    other = lax.ppermute(own, "core", SWAP)
    order = jnp.stack(
        [
            (at_xh if k == 0 else 1 - at_xh) * ys + (at_y + by) % ys
            for by in (0, ys - 1, 1, 2)
            for k in (0, 1)
        ]
    ).astype(jnp.int32)

    combined = mirror(grouped, occupied)
    combined_x = lax.ppermute(combined, "xl", SWAP)
    combined_local = lax.all_to_all(combined, PAIR, split_axis=0, concat_axis=1, tiled=True)
    combined_local = combined_local.reshape(pair_count, slab_width, full_width)

    hole_sent = hole_rows(order, own, other, combined_x)
    hole_got = lax.ppermute(hole_sent, "xl", SWAP)
    hole_own = hole_rows(order, own, other, combined)
    by_core = jnp.stack([hole_own, hole_got])
    by_core = jnp.where(at_core == 1, by_core[:, ::-1], by_core)
    by_xl = jnp.where(at_xl == 1, by_core[::-1], by_core)
    hole = by_xl.reshape(pair_count, groups, columns).transpose(1, 0, 2)
    hole = hole.reshape(pairs, columns)
    hole_local = lax.all_to_all(hole, PAIR, split_axis=0, concat_axis=1, tiled=True)
    hole_local = hole_local.reshape(pair_count, slab_width, full_width)

    packed = jnp.concatenate([combined_local, fock_virtual[None]], axis=0)
    packed_c = lax.ppermute(packed, "core", SWAP)
    packed_x = lax.ppermute(packed, "xl", SWAP)
    packed_xc = lax.ppermute(packed_x, "core", SWAP)

    near = flip_if(at_core == 1, packed, packed_c)
    far = flip_if(at_core == 1, packed_x, packed_xc)
    low0, high0 = flip_if(at_xl == 1, near[0], far[0])
    low1, high1 = flip_if(at_xl == 1, near[1], far[1])
    whole = jnp.concatenate([low0, low1, high0, high1], axis=1)
    fock_full = whole[pair_count]
    first_term = dot(
        jnp.broadcast_to(fock_virtual, (pair_count,) + fock_virtual.shape),
        whole[:pair_count],
        (((2,), (1,)), ((0,), (0,))),
        FAST,
    )
    second_term = dot(combined_local, fock_full, (((2,), (1,)), ((), ())), FAST)
    residual = first_term + second_term + hole_local

    pair_base = lax.axis_index(PAIR) * pair_count
    pair_ids = pair_base + jnp.arange(pair_count, dtype=jnp.int32)
    orbital_ids = jnp.arange(occupied, dtype=jnp.int32)
    left_pick = pair_ids[:, None] // occupied == orbital_ids[None, :]
    right_pick = pair_ids[:, None] % occupied == orbital_ids[None, :]
    left_energy = jnp.sum(jnp.where(left_pick, occupied_energy[None, :], jnp.float32(0.0)), axis=1)
    right_energy = jnp.sum(
        jnp.where(right_pick, occupied_energy[None, :], jnp.float32(0.0)), axis=1
    )
    slab_energy = lax.dynamic_slice_in_dim(
        virtual_energy, lax.axis_index(("xl", "core")) * slab_width, slab_width
    )
    denominator = (
        (left_energy + right_energy)[:, None, None]
        - slab_energy[None, :, None]
        - virtual_energy[None, None, :]
    )
    return residual / denominator


def solution(mesh):
    fine = Mesh(
        mesh.devices.reshape(16, 2, 4, 2, 2), ("z", "xh", "y", "xl", "core")
    )
    virt = ("xl", "core")
    return jax.shard_map(
        shards,
        mesh=fine,
        in_specs=(P(PAIR, virt, None), P(virt, None), P(PAIR + virt, None), P(), P()),
        out_specs=P(PAIR, virt, None),
        check_vma=False,
    )
```

```python
import jax
import jax.numpy as jnp
from jax import lax
from jax.experimental import pallas as pl
from jax.experimental.pallas import tpu as pltpu
from jax.sharding import Mesh, PartitionSpec as P

FAST = lax.Precision.HIGH
PAIR = ("z", "xh", "y")
SWAP = [(0, 1), (1, 0)]


def dot(a, b, dims, precision):
    return lax.dot_general(a, b, dims, precision=precision, preferred_element_type=jnp.float32)


def mirror(grouped, occupied):
    columns = grouped.shape[1]
    shaped = grouped.reshape(occupied, occupied, columns)
    return (2.0 * shaped - jnp.transpose(shaped, (1, 0, 2))).reshape(occupied * occupied, columns)


def flip_if(flag, first, second):
    return jnp.where(flag, second, first), jnp.where(flag, first, second)


def split(value):
    high = value.astype(jnp.bfloat16)
    return high, (value - high.astype(jnp.float32)).astype(jnp.bfloat16)


def hole_kernel(order_ref, own_ref, other_ref, combined_ref, out_ref, high_ref, low_ref):
    chunks = own_ref.shape[0]
    depth = own_ref.shape[2]
    for k in range(chunks):
        start = pl.multiple_of(order_ref[k] * depth, depth)
        high, low = split(combined_ref[pl.ds(start, depth), :])
        high_ref[k * depth : (k + 1) * depth, :] = high
        low_ref[k * depth : (k + 1) * depth, :] = low
    for half, ref in enumerate((own_ref, other_ref)):
        rows = jnp.concatenate([ref[k] for k in range(chunks)], axis=1)
        high, low = split(rows)
        total = jnp.dot(low, high_ref[...], preferred_element_type=jnp.float32)
        total += jnp.dot(high, low_ref[...], preferred_element_type=jnp.float32)
        total += jnp.dot(high, high_ref[...], preferred_element_type=jnp.float32)
        out_ref[half] = total


def hole_rows(order, own, other, combined):
    chunks, rows, depth = own.shape
    columns = combined.shape[1]
    vmem = pl.BlockSpec(memory_space=pltpu.VMEM)
    flops = 12 * rows * chunks * depth * columns
    return pl.pallas_call(
        hole_kernel,
        out_shape=jax.ShapeDtypeStruct((2, rows, columns), jnp.float32),
        in_specs=[pl.BlockSpec(memory_space=pltpu.SMEM), vmem, vmem, vmem],
        out_specs=vmem,
        scratch_shapes=[pltpu.VMEM((chunks * depth, columns), jnp.bfloat16)] * 2,
        compiler_params=pltpu.CompilerParams(vmem_limit_bytes=16 << 20),
        cost_estimate=pl.CostEstimate(
            flops=flops, bytes_accessed=4 * (2 * own.size + combined.size), transcendentals=0
        ),
    )(order, own, other, combined)


def shards(amplitudes, fock_virtual, hole_ladder, occupied_energy, virtual_energy):
    pair_count, slab_width, full_width = amplitudes.shape
    occupied = occupied_energy.shape[0]
    pairs = occupied * occupied
    zs, xhs, ys = lax.axis_size("z"), lax.axis_size("xh"), lax.axis_size("y")
    plane = xhs * ys
    groups = zs * plane
    at_xh, at_y = lax.axis_index("xh"), lax.axis_index("y")
    at_xl, at_core = lax.axis_index("xl"), lax.axis_index("core")
    columns = slab_width * full_width // groups
    ladder_rows = hole_ladder.shape[0]
    depth = pairs // plane

    outgoing = amplitudes.reshape(pair_count, groups, columns).transpose(1, 0, 2)
    outgoing = outgoing.reshape(groups, pair_count * columns)
    rungs = hole_ladder.reshape(ladder_rows, plane, depth).transpose(1, 0, 2)
    rungs = jnp.tile(rungs.reshape(plane, ladder_rows * depth), (zs, 1))
    sent = jnp.concatenate([outgoing, rungs], axis=1)[:, None, :]
    arrived = lax.all_to_all(sent, PAIR, split_axis=0, concat_axis=0, tiled=True)[:, 0, :]
    grouped = arrived[:, : pair_count * columns].reshape(pairs, columns)
    rungs = arrived[:, pair_count * columns :].reshape(groups, ladder_rows, depth)
    rungs = rungs.transpose(1, 0, 2).reshape(ladder_rows * groups, depth)

    both = jnp.stack([rungs, lax.ppermute(rungs, "xh", SWAP)])
    shift = lambda by: [(i, (i + by) % ys) for i in range(ys)]
    quads = [both] + [lax.ppermute(both, "y", shift(by)) for by in (1, ys - 1, 2)]
    own = jnp.concatenate(quads, axis=0)
    other = lax.ppermute(own, "core", SWAP)
    order = jnp.stack(
        [
            (at_xh if k == 0 else 1 - at_xh) * ys + (at_y + by) % ys
            for by in (0, ys - 1, 1, 2)
            for k in (0, 1)
        ]
    ).astype(jnp.int32)

    combined = mirror(grouped, occupied)
    combined_x = lax.ppermute(combined, "xl", SWAP)
    combined_local = lax.all_to_all(combined, PAIR, split_axis=0, concat_axis=1, tiled=True)
    combined_local = combined_local.reshape(pair_count, slab_width, full_width)

    hole_sent = hole_rows(order, own, other, combined_x)
    hole_got = lax.ppermute(hole_sent, "xl", SWAP)
    hole_own = hole_rows(order, own, other, combined)
    hole = jnp.stack([hole_own, hole_got]).reshape(pair_count, groups, columns)
    hole = hole.transpose(1, 0, 2)
    returned = lax.all_to_all(hole, PAIR, split_axis=0, concat_axis=0, tiled=True)

    packed = jnp.concatenate([combined_local, fock_virtual[None]], axis=0)
    packed_x = lax.ppermute(packed, "xl", SWAP)
    packed_c = lax.ppermute(packed, "core", SWAP)
    packed_xc = lax.ppermute(packed_x, "core", SWAP)

    near = flip_if(at_core == 1, packed, packed_c)
    far = flip_if(at_core == 1, packed_x, packed_xc)
    low0, high0 = flip_if(at_xl == 1, near[0], far[0])
    low1, high1 = flip_if(at_xl == 1, near[1], far[1])
    whole = jnp.concatenate([low0, low1, high0, high1], axis=1)
    fock_full = whole[pair_count]
    first_term = dot(
        jnp.broadcast_to(fock_virtual, (pair_count,) + fock_virtual.shape),
        whole[:pair_count],
        (((2,), (1,)), ((0,), (0,))),
        FAST,
    )
    second_term = dot(combined_local, fock_full, (((2,), (1,)), ((), ())), FAST)
    particle = lax.optimization_barrier(first_term + second_term)

    pair_base = lax.axis_index(PAIR) * pair_count
    pair_ids = pair_base + jnp.arange(pair_count, dtype=jnp.int32)
    orbital_ids = jnp.arange(occupied, dtype=jnp.int32)
    left_pick = pair_ids[:, None] // occupied == orbital_ids[None, :]
    right_pick = pair_ids[:, None] % occupied == orbital_ids[None, :]
    left_energy = jnp.sum(jnp.where(left_pick, occupied_energy[None, :], jnp.float32(0.0)), axis=1)
    right_energy = jnp.sum(
        jnp.where(right_pick, occupied_energy[None, :], jnp.float32(0.0)), axis=1
    )
    slab_energy = lax.dynamic_slice_in_dim(
        virtual_energy, lax.axis_index(("xl", "core")) * slab_width, slab_width
    )
    pair_energy = left_energy + right_energy
    virtual_pair = slab_energy[:, None] + virtual_energy[None, :]
    flip = (2 * at_xl + at_core) * (pair_count // 4)
    slots = jnp.bitwise_xor(jnp.arange(pair_count, dtype=jnp.int32), flip.astype(jnp.int32))
    return finish(slots, pair_energy, returned, particle, virtual_pair)


def finish_kernel(slots_ref, energy_ref, hole_ref, particle_ref, virtual_ref, out_ref):
    pair_count, slab_width, full_width = out_ref.shape
    lanes = hole_ref.shape[1]
    pieces = full_width // lanes
    stride = pieces * pair_count
    for place in range(pair_count):
        slot = slots_ref[place]
        energy = energy_ref[slot]
        for piece in range(pieces):
            first = piece * pair_count + place
            hole = hole_ref[pl.ds(first, slab_width, stride=stride), :]
            cols = slice(piece * lanes, (piece + 1) * lanes)
            residual = particle_ref[slot, :, cols] + hole
            out_ref[slot, :, cols] = residual / (energy - virtual_ref[:, cols])


def finish(slots, pair_energy, returned, particle, virtual_pair):
    groups, pair_count, lanes = returned.shape
    smem = pl.BlockSpec(memory_space=pltpu.SMEM)
    vmem = pl.BlockSpec(memory_space=pltpu.VMEM)
    return pl.pallas_call(
        finish_kernel,
        out_shape=jax.ShapeDtypeStruct(particle.shape, jnp.float32),
        in_specs=[smem, smem, vmem, vmem, vmem],
        out_specs=vmem,
        compiler_params=pltpu.CompilerParams(vmem_limit_bytes=8 << 20),
        cost_estimate=pl.CostEstimate(
            flops=4 * particle.size, bytes_accessed=12 * particle.size, transcendentals=0
        ),
    )(slots, pair_energy, returned.reshape(groups * pair_count, lanes), particle, virtual_pair)


def solution(mesh):
    fine = Mesh(
        mesh.devices.reshape(16, 2, 4, 2, 2), ("z", "xh", "y", "xl", "core")
    )
    virt = ("xl", "core")
    return jax.shard_map(
        shards,
        mesh=fine,
        in_specs=(P(PAIR, virt, None), P(virt, None), P(PAIR + virt, None), P(), P()),
        out_specs=P(PAIR, virt, None),
        check_vma=False,
    )
```
